32 devices in a mesh: row: 4 (over x, core), col: 8 (over z, y).
Axes of the slice: x: 2, y: 2, z: 4, core: 2. Of those that a mesh axis runs over, the one named last changes fastest.
Arguments:
- pair: bfloat16 [8, 4, 2, 64, 128], P(None, 'row', None, 'col'), may hold values from -5 to 5
- w_query: bfloat16 [2, 2, 128, 256], replicated, may hold values from -4 to 4
- w_key: bfloat16 [2, 2, 128, 256], replicated, may hold values from -4 to 4
- w_value: bfloat16 [2, 2, 128, 256], replicated, may hold values from -0.5 to 0.5
- w_gate: bfloat16 [2, 2, 128, 256], replicated, may hold values from -0.5 to 0.5
- w_out: bfloat16 [2, 2, 256, 128], replicated, may hold values from -3 to 3
- w_in: bfloat16 [2, 128, 512], replicated, may hold values from -0.5 to 0.5
- w_back: bfloat16 [2, 512, 128], replicated, may hold values from -0.25 to 0.25
Outputs:
- pair_out: bfloat16 [8, 4, 2, 64, 128], P(None, 'row', None, 'col')
The draws below stay inside these ranges and needn't reach their ends.
All inputs are finite; a program needn't handle non-finite values.
Results may differ from the reference program's by a relative error of at most 0.03.
Values may be sent and summed in bfloat16 or wider, within the bound.
No kernel may reach another device: no remote copies, remote signals or barrier semaphores. Data moves between devices by JAX's collectives and lax.ppermute only.
A program may use at most 64 MiB of HBM per device.

```python
from functools import partial
import jax
import jax.numpy as jnp
from jax import lax

CHANNELS = 128
HEADS = 8
HEAD_DIM = 32
FF_UNITS = 512
LAYERS = 2
SPAN = 2
GROUPS = 4
BLOCKS = 8
RESIDUES = 64
INNER = 256


def draw_pair(key, part):
    full_grid = jax.random.normal(jax.random.fold_in(key, 11), (RESIDUES, RESIDUES, CHANNELS), jnp.float32)
    full_grid = jnp.clip(full_grid, -5.0, 5.0)
    return full_grid.reshape(BLOCKS, GROUPS, SPAN, RESIDUES, CHANNELS).astype(jnp.bfloat16)


def query_key_pair(key):
    full_shape = (LAYERS, 2, CHANNELS, HEADS, HEAD_DIM)
    spread = CHANNELS ** (-0.5)
    first_draw = jax.random.normal(jax.random.fold_in(key, 21), full_shape, jnp.float32) * spread
    second_draw = jax.random.normal(jax.random.fold_in(key, 22), full_shape, jnp.float32) * spread
    first_draw = jnp.clip(first_draw, -4.0, 4.0).reshape(LAYERS, 2, CHANNELS, HEADS * HEAD_DIM)
    second_draw = jnp.clip(second_draw, -4.0, 4.0).reshape(LAYERS, 2, CHANNELS, HEADS * HEAD_DIM)
    return (first_draw, second_draw)


def draw_w_query(key, part):
    return query_key_pair(key)[0].astype(jnp.bfloat16)


def draw_w_key(key, part):
    return query_key_pair(key)[1].astype(jnp.bfloat16)


def normal_values(own_key, extent, scale, bound, dtype=jnp.bfloat16):
    array = scale * jax.random.normal(own_key, extent, jnp.float32)
    return jnp.clip(array, min=-bound, max=bound).astype(dtype)


def setup_inputs(seed: int = 0) -> dict:
    seeds = jax.random.split(jax.random.key(seed), 9)
    pair = draw_pair(jax.random.fold_in(seeds[8], 71), 0)
    w_query = draw_w_query(jax.random.fold_in(seeds[8], 71), 0)
    w_key = draw_w_key(jax.random.fold_in(seeds[8], 71), 0)
    w_value = normal_values(seeds[3], (LAYERS, 2, CHANNELS, INNER), CHANNELS ** -0.5, 0.5)
    w_gate = normal_values(seeds[4], (LAYERS, 2, CHANNELS, INNER), CHANNELS ** -0.5, 0.5)
    w_out = normal_values(seeds[5], (LAYERS, 2, INNER, CHANNELS), 0.5, 3.0)
    w_in = normal_values(seeds[6], (LAYERS, CHANNELS, FF_UNITS), CHANNELS ** -0.5, 0.5)
    w_back = normal_values(seeds[7], (LAYERS, FF_UNITS, CHANNELS), FF_UNITS ** -0.5, 0.25)
    return dict(pair=pair, w_query=w_query, w_key=w_key, w_value=w_value, w_gate=w_gate, w_out=w_out, w_in=w_in, w_back=w_back)


epsilon = 1e-05

def rounded(values):
    return lax.optimization_barrier(values.astype(jnp.bfloat16))

def layer_norm(values):
    wide = values.astype(jnp.float32)
    center = wide - lax.optimization_barrier(jnp.mean(wide, axis=-1, keepdims=True))
    spread = lax.optimization_barrier(jnp.mean(center * center, axis=-1, keepdims=True))
    return rounded(center * lax.rsqrt(spread + epsilon))

def split_heads(matrix):
    return matrix.reshape(matrix.shape[0], HEADS, matrix.shape[1] // HEADS).astype(jnp.float32)

def one_row(normed, weights):
    wide = normed.astype(jnp.float32)
    queries = rounded(jnp.einsum('qc,chd->hqd', wide, split_heads(weights[0])))
    key_rows = rounded(jnp.einsum('qc,chd->hqd', wide, split_heads(weights[1])))
    value_rows = rounded(jnp.einsum('qc,chd->hqd', wide, split_heads(weights[2])))
    gating = jax.nn.sigmoid(jnp.einsum('qc,chd->hqd', wide, split_heads(weights[3])))
    scores = jnp.einsum('hqd,hkd->hqk', queries.astype(jnp.float32), key_rows.astype(jnp.float32)) * HEAD_DIM ** (-0.5)
    maximum = lax.optimization_barrier(jnp.max(scores, axis=-1, keepdims=True))
    exponent = jnp.exp(scores - maximum)
    denominator = lax.optimization_barrier(jnp.sum(exponent, axis=-1, keepdims=True))
    probs = rounded(exponent)
    blended = jnp.einsum('hqk,hkd->hqd', probs.astype(jnp.float32), value_rows.astype(jnp.float32)) / denominator
    gated_out = rounded(gating * blended)
    out_heads = weights[4].reshape(HEADS, HEAD_DIM, CHANNELS).astype(jnp.float32)
    return jnp.einsum('hqd,hdc->qc', gated_out.astype(jnp.float32), out_heads)

def attend_rows(grid, weights):
    normed = layer_norm(grid)
    update = lax.map(partial(one_row, weights=weights), normed)
    return rounded(grid.astype(jnp.float32) + update)

def reference(pair, w_query, w_key, w_value, w_gate, w_out, w_in, w_back):
    grid = pair.reshape(RESIDUES, RESIDUES, CHANNELS)

    def layer_step(grid, layer_weights):
        row_mats = tuple((matrix[0] for matrix in layer_weights[:5]))
        col_mats = tuple((matrix[1] for matrix in layer_weights[:5]))
        grid = attend_rows(grid, row_mats)
        flipped = jnp.swapaxes(grid, 0, 1)
        grid = jnp.swapaxes(attend_rows(flipped, col_mats), 0, 1)
        symmetric = rounded(0.5 * (grid.astype(jnp.float32) + jnp.swapaxes(grid, 0, 1).astype(jnp.float32)))
        normed = layer_norm(symmetric).reshape(RESIDUES * RESIDUES, CHANNELS)
        hidden = rounded(jax.nn.relu(jnp.dot(normed, layer_weights[5], preferred_element_type=jnp.float32)))
        ff_out = jnp.dot(hidden, layer_weights[6], preferred_element_type=jnp.float32)
        flat = symmetric.reshape(RESIDUES * RESIDUES, CHANNELS).astype(jnp.float32)
        grid = rounded(flat + ff_out).reshape(RESIDUES, RESIDUES, CHANNELS)
        return (grid, None)
    final_grid, unused = lax.scan(layer_step, grid, (w_query, w_key, w_value, w_gate, w_out, w_in, w_back))
    return final_grid.reshape(pair.shape)
```

```python
import functools
import math

import jax
import jax.numpy as jnp
from jax import lax
from jax.experimental import pallas as pl
from jax.experimental.pallas import tpu as pltpu
from jax.sharding import PartitionSpec as P

HEADS = 8
HEAD_DIM = 32
LANES = 128
VMEM_BUDGET = 24 * 2**20


epsilon = 1e-05


def layer_norm(values):
    wide = values.astype(jnp.float32)
    center = wide - jnp.mean(wide, axis=-1, keepdims=True)
    spread = jnp.mean(center * center, axis=-1, keepdims=True)
    return (center * lax.rsqrt(spread + epsilon)).astype(jnp.bfloat16)


def split_heads(matrix):
    return matrix.reshape(matrix.shape[0], HEADS, matrix.shape[1] // HEADS)


def attend(normed, weights, direction, pattern):
    project = pattern + ",chd->ehqd"
    queries = jnp.einsum(
        project, normed, split_heads(weights[0][direction]), preferred_element_type=jnp.float32
    ).astype(jnp.bfloat16)
    key_rows = jnp.einsum(
        project, normed, split_heads(weights[1][direction]), preferred_element_type=jnp.float32
    ).astype(jnp.bfloat16)
    value_rows = jnp.einsum(
        project, normed, split_heads(weights[2][direction]), preferred_element_type=jnp.float32
    ).astype(jnp.bfloat16)
    gating = jax.nn.sigmoid(
        jnp.einsum(
            project, normed, split_heads(weights[3][direction]), preferred_element_type=jnp.float32
        )
    )
    scores = jnp.einsum(
        "ehqd,ehkd->ehqk", queries, key_rows, preferred_element_type=jnp.float32
    ) * HEAD_DIM ** (-0.5)
    maximum = jnp.max(scores, axis=-1, keepdims=True)
    exponent = jnp.exp(scores - maximum)
    denominator = jnp.sum(exponent, axis=-1, keepdims=True)
    blended = (
        jnp.einsum(
            "ehqk,ehkd->ehqd",
            exponent.astype(jnp.bfloat16),
            value_rows,
            preferred_element_type=jnp.float32,
        )
        / denominator
    )
    gated_out = (gating * blended).astype(jnp.bfloat16)
    out_matrix = weights[4][direction]
    out_heads = out_matrix.reshape(HEADS, out_matrix.shape[0] // HEADS, out_matrix.shape[1])
    return jnp.einsum(
        "ehqd,hdc->" + pattern, gated_out, out_heads, preferred_element_type=jnp.float32
    )


def local_slabs(pair, w_query, w_key, w_value, w_gate, w_out, w_in, w_back):
    row_count = lax.axis_size("row")
    col_count = lax.axis_size("col")
    span_rows = pair.shape[2]
    col_width = pair.shape[3]
    channels = pair.shape[4]
    length = col_count * col_width
    pair_tile = pair.reshape(col_count, span_rows, col_width, channels)

    def layer_step(pair_tile, layer_weights):
        attn_weights = layer_weights[:5]
        row_slab = lax.all_to_all(
            pair_tile, "col", split_axis=0, concat_axis=2, tiled=True
        ).reshape(span_rows, length, channels)
        row_update = attend(layer_norm(row_slab), attn_weights, 0, "eqc")
        row_slab = (row_slab.astype(jnp.float32) + row_update).astype(jnp.bfloat16)
        pair_tile = lax.all_to_all(
            row_slab.reshape(1, span_rows, length, channels),
            "col",
            split_axis=2,
            concat_axis=0,
            tiled=True,
        )
        pair_tile = pair_tile.reshape(col_count, span_rows, row_count, span_rows, channels)
        col_slab = lax.all_to_all(pair_tile, "row", split_axis=2, concat_axis=1, tiled=True)
        col_slab = col_slab.reshape(length, span_rows, channels)
        col_update = attend(layer_norm(col_slab), attn_weights, 1, "qec")
        col_slab = (col_slab.astype(jnp.float32) + col_update).astype(jnp.bfloat16)
        pair_tile = lax.all_to_all(
            col_slab.reshape(col_count, row_count * span_rows, 1, span_rows, channels),
            "row",
            split_axis=1,
            concat_axis=2,
            tiled=True,
        )
        pair_tile = pair_tile.reshape(col_count, span_rows, col_width, channels)
        mirrored = lax.all_to_all(
            col_slab.reshape(col_count, col_width, span_rows, channels),
            "col",
            split_axis=0,
            concat_axis=2,
            tiled=True,
        )
        mirrored = jnp.transpose(
            mirrored.reshape(col_width, col_count * span_rows, channels), (1, 0, 2)
        )
        mirrored = mirrored.reshape(col_count, span_rows, col_width, channels)
        symmetric = (0.5 * (pair_tile.astype(jnp.float32) + mirrored.astype(jnp.float32))).astype(
            jnp.bfloat16
        )
        normed = layer_norm(symmetric)
        hidden = jax.nn.relu(
            jnp.einsum(
                "aewc,cf->aewf", normed, layer_weights[5], preferred_element_type=jnp.float32
            )
        ).astype(jnp.bfloat16)
        ff_out = jnp.einsum(
            "aewf,fc->aewc", hidden, layer_weights[6], preferred_element_type=jnp.float32
        )
        pair_tile = (symmetric.astype(jnp.float32) + ff_out).astype(jnp.bfloat16)
        return (pair_tile, None)

    final_tile, unused = lax.scan(
        layer_step, pair_tile, (w_query, w_key, w_value, w_gate, w_out, w_in, w_back)
    )
    return final_tile.reshape(pair.shape)


def dot(left, right, contract=((1,), (0,))):
    return lax.dot_general(left, right, (contract, ((), ())), preferred_element_type=jnp.float32)


NT = ((1,), (1,))
TN = ((0,), (0,))


def project(normed, span, weights, stores):
    w_query, w_key, w_value_gate = weights
    queries, keys, values, gates = stores
    inner = w_query.shape[1]
    queries[span, :] = dot(normed, w_query[...]).astype(jnp.bfloat16)
    keys[span, :] = dot(normed, w_key[...]).astype(jnp.bfloat16)
    values[:, span] = dot(w_value_gate[:inner, :], normed, NT).astype(jnp.bfloat16)
    gates[:, span] = jax.nn.sigmoid(dot(w_value_gate[inner:, :], normed, NT))


def attend_pair(start, length, stores, w_out):
    queries, keys, values, gates = stores
    both = pl.ds(start, 2 * length)
    per_group = LANES // HEAD_DIM
    groups = HEADS // per_group
    scale = HEAD_DIM ** (-0.5) * math.log2(math.e)
    lane = lax.broadcasted_iota(jnp.int32, (1, LANES), 1)
    head_masks = [
        (lane // HEAD_DIM == h).astype(jnp.float32).astype(jnp.bfloat16) for h in range(per_group)
    ]
    low = lane < length
    low_mask = low.astype(jnp.float32).astype(jnp.bfloat16)
    high_mask = (~low).astype(jnp.float32).astype(jnp.bfloat16)
    gated = [None] * HEADS
    for group in range(groups):
        channels = slice(group * LANES, (group + 1) * LANES)
        probs, denominators = [], []
        for which in range(2):
            rows = pl.ds(start + which * length, length)
            query = queries[rows, channels]
            order = [h ^ which for h in range(per_group)]
            spread = jnp.concatenate([query * head_masks[h] for h in order], axis=0)
            scores = dot(keys[rows, channels], spread, NT)
            exponent = jnp.exp2((scores - jnp.max(scores, axis=0, keepdims=True)) * scale)
            denominators.append(jnp.sum(exponent, axis=0, keepdims=True))
            probs.append(exponent.astype(jnp.bfloat16))
        for tile in range(per_group // 2):
            columns = slice(tile * LANES, (tile + 1) * LANES)
            first, second = probs[0][:, columns], probs[1][:, columns]
            spread = jnp.concatenate(
                [
                    jnp.concatenate([first * low_mask, second * high_mask], axis=0),
                    jnp.concatenate([first * high_mask, second * low_mask], axis=0),
                ],
                axis=1,
            )
            head = group * per_group + 2 * tile
            inner = slice(head * HEAD_DIM, (head + 2) * HEAD_DIM)
            blended = dot(values[inner, both], spread)
            one, two = denominators[0][:, columns], denominators[1][:, columns]
            even = blended[:HEAD_DIM, :LANES] / jnp.where(low, one, two)
            odd = blended[HEAD_DIM:, LANES:] / jnp.where(low, two, one)
            odd = pltpu.roll(odd, length, 1)
            gate = gates[inner, both]
            gated[head] = (gate[:HEAD_DIM] * even).astype(jnp.bfloat16)
            gated[head + 1] = (gate[HEAD_DIM:] * odd).astype(jnp.bfloat16)
    return dot(jnp.concatenate(gated, axis=0), w_out[...], TN)


def rounded(values):
    return values.astype(jnp.bfloat16).astype(jnp.float32)


def attend_slab(grid, length, stores, w_out, unroll):
    pair = 2 * length

    def step(index, carry):
        start = pl.multiple_of(index * pair, pair)
        update = attend_pair(start, length, stores, w_out)
        here = pl.ds(start, pair)
        grid[here, :] = rounded(grid[here, :] + update)
        return carry

    lax.fori_loop(0, grid.shape[0] // pair, step, 0, unroll=unroll)


def transition(values, w_in, w_back):
    hidden = jnp.maximum(dot(layer_norm(values), w_in[...]), 0.0).astype(jnp.bfloat16)
    return rounded(values + dot(hidden, w_back[...]))


def first_row_kernel(dims, *refs):
    blocks, pairs, span, width = dims
    parts = refs[:4]
    w_query, w_key, w_value_gate, w_out, keep, send, grid = refs[4:11]
    stores = refs[11:15]
    row, col = lax.axis_index("row"), lax.axis_index("col")
    x, core = row // 2, row % 2
    length = blocks * width
    half = blocks * pairs * span
    for number, part in enumerate(parts):
        dx, dy = number // 2, number % 2
        at_x = x ^ dx
        for other in range(blocks // 2):
            at_c = col ^ (2 * other + dy)
            for a in range(blocks):
                for e in range(span):
                    at = ((a * pairs + at_x) * span + e) * length + at_c * width
                    grid[pl.ds(pl.multiple_of(at, width), width), :] = part[other, a, e].astype(
                        jnp.float32
                    )
    chunk = 4 * length

    def step(index, carry):
        here = pl.ds(pl.multiple_of(index * chunk, chunk), chunk)
        project(layer_norm(grid[here, :]), here, (w_query, w_key, w_value_gate), stores)
        return carry

    lax.fori_loop(0, grid.shape[0] // chunk, step, 0)
    attend_slab(grid, length, stores, w_out, 2)
    for target, parity in ((keep, core), (send, 1 - core)):
        for a in range(blocks):
            for other in range(pairs):
                for e in range(span):
                    at = a * width + other * 2 * span + parity * span + e
                    target[(a * pairs + other) * span + e] = grid[
                        pl.ds(at, half, stride=length), :
                    ].astype(jnp.bfloat16)


def col_kernel(keep, recv, w_query, w_key, w_value_gate, w_out, slab, own, send, grid, *stores):
    half = keep.shape[1]
    length = 2 * half
    count = 4

    def step(index, carry):
        seqs = pl.ds(index * count, count)
        values = jnp.concatenate([keep[seqs], recv[seqs]], axis=1).astype(jnp.float32)
        values = values.reshape(count * length, values.shape[2])
        here = pl.ds(pl.multiple_of(index * count * length, count * length), count * length)
        grid[here, :] = values
        project(layer_norm(values), here, (w_query, w_key, w_value_gate), stores)
        return carry

    lax.fori_loop(0, half // count, step, 0)
    attend_slab(grid, length, stores, w_out, 2)
    for j in range(half):
        slab[j] = grid[j * length : (j + 1) * length, :].astype(jnp.bfloat16)
    for i in range(half):
        own[i] = grid[pl.ds(i, half, stride=length), :].astype(jnp.bfloat16)
        send[i] = grid[pl.ds(half + i, half, stride=length), :].astype(jnp.bfloat16)


def mid_row_kernel(
    dims, slab, own, recv, w_in, w_back, w_query, w_key, w_value_gate, w_out, keep, send, grid, *stores
):
    blocks, pairs, span, width = dims
    half = own.shape[0]
    length = 2 * half
    count = 4
    row, col = lax.axis_index("row"), lax.axis_index("col")
    x, core = row // 2, row % 2

    def step(index, carry):
        seqs = pl.ds(index * count, count)
        direct = jnp.concatenate([own[seqs], recv[seqs]], axis=1).astype(jnp.float32)
        values = rounded(0.5 * (direct + slab[seqs].astype(jnp.float32)))
        values = transition(values.reshape(count * length, values.shape[2]), w_in, w_back)
        here = pl.ds(pl.multiple_of(index * count * length, count * length), count * length)
        grid[here, :] = values
        project(layer_norm(values), here, (w_query, w_key, w_value_gate), stores)
        return carry

    lax.fori_loop(0, half // count, step, 0)
    attend_slab(grid, length, stores, w_out, 2)
    for other in range(pairs):
        for k in range(2):
            for e in range(span):
                number = (other * 2 + k) * span + e
                inside = (col * pairs + other) * span + e
                for target, mine in ((keep, core), (send, 1 - core)):
                    at = inside + half * (k ^ mine)
                    if target is send:
                        at = inside + half * (k ^ core)
                    else:
                        at = inside + half * (k ^ core)
                    target[number] = grid[pl.ds(at, half, stride=length), :].astype(jnp.bfloat16)
    for a in range(blocks):
        for e in range(span):
            inside = (a * pairs + x) * span + e
            number = width + a * span + e
            keep[number] = grid[pl.ds(inside, half, stride=length), :].astype(jnp.bfloat16)
            send[number] = grid[pl.ds(half + inside, half, stride=length), :].astype(jnp.bfloat16)


def few_queries(query, keys, values, head_masks, tile_masks):
    scale = HEAD_DIM ** (-0.5) * math.log2(math.e)
    count = query.shape[0]
    spread = jnp.concatenate([query * mask for mask in head_masks], axis=0)
    scores = dot(spread, keys, NT)
    exponent = jnp.exp2((scores - jnp.max(scores, axis=1, keepdims=True)) * scale)
    denominator = jnp.sum(exponent, axis=1, keepdims=True)
    blended = dot(exponent.astype(jnp.bfloat16), values) / denominator
    total = None
    for h in range(HEADS):
        term = blended[h * count : (h + 1) * count] * tile_masks[h]
        total = term if total is None else total + term
    return total


def last_kernel(
    dims, keep, recv, w_query, w_key, w_value, w_gate, w_out, w_in, w_back, out, grid, keys, values, picked, blended
):
    blocks, pairs, span, width = dims
    half = keep.shape[1]
    length = 2 * half
    seqs = keep.shape[0]
    row, col = lax.axis_index("row"), lax.axis_index("col")
    x, core = row // 2, row % 2
    tall = blocks * span
    tile = width * tall
    chunk = 8
    for index in range(seqs // chunk):
        part = slice(index * chunk, (index + 1) * chunk)
        wide = jnp.concatenate([keep[part], recv[part]], axis=1).astype(jnp.float32)
        wide = wide.reshape(chunk * length, wide.shape[2])
        here = slice(index * chunk * length, (index + 1) * chunk * length)
        grid[here, :] = wide
        normed = layer_norm(wide)
        keys[here, :] = dot(normed, w_key[...]).astype(jnp.bfloat16)
        values[here, :] = dot(normed, w_value[...]).astype(jnp.bfloat16)
    for w in range(width):
        for e in range(span):
            at = w * length + x * span + e
            picked[pl.ds((w * span + e) * blocks, blocks), :] = grid[
                pl.ds(at, blocks, stride=pairs * span), :
            ]
    for a in range(blocks):
        for e in range(span):
            seq = width + a * span + e
            for other in range(pairs):
                for k in range(2):
                    for e2 in range(span):
                        w = (other * 2 + k) * span + e2
                        at = seq * length + half * (k ^ core) + (col * pairs + other) * span + e2
                        picked[pl.ds(tile + (e * blocks + a) * width + w, 1), :] = grid[
                            pl.ds(at, 1), :
                        ]
    here = picked[...]
    normed = layer_norm(here)
    queries = dot(normed, w_query[...]).astype(jnp.bfloat16)
    gating = jax.nn.sigmoid(dot(normed, w_gate[...]))
    inner = queries.shape[1]
    lane = lax.broadcasted_iota(jnp.int32, (1, inner), 1)
    tile_masks = [(lane // HEAD_DIM == h).astype(jnp.float32) for h in range(HEADS)]
    head_masks = [mask.astype(jnp.bfloat16) for mask in tile_masks]
    for w in range(width):
        rows = slice(w * tall, (w + 1) * tall)
        at = slice(w * length, (w + 1) * length)
        blended[rows, :] = few_queries(queries[rows], keys[at, :], values[at, :], head_masks, tile_masks)
    for a in range(blocks):
        for e in range(span):
            start = tile + (e * blocks + a) * width
            seq = width + a * span + e
            rows = slice(start, start + width)
            at = slice(seq * length, (seq + 1) * length)
            blended[rows, :] = few_queries(
                queries[rows], keys[at, :], values[at, :], head_masks, tile_masks
            )
    gated = (gating * blended[...]).astype(jnp.bfloat16)
    picked[...] = rounded(here + dot(gated, w_out[...]))
    for e in range(span):
        for a in range(blocks):
            start = (e * blocks + a) * width
            direct = picked[pl.ds(e * blocks + a, width, stride=tall), :]
            mirrored = picked[tile + start : tile + start + width, :]
            grid[start : start + width, :] = rounded(0.5 * (direct + mirrored))
    result = transition(grid[:tile, :], w_in, w_back)
    for e in range(span):
        for a in range(blocks):
            start = (e * blocks + a) * width
            out[a, 0, e] = result[start : start + width].astype(jnp.bfloat16)


def whole(shape):
    return pl.BlockSpec(shape, lambda i: (0,) * len(shape))


def part_of(array, layer, direction=None):
    lead = (layer,) if direction is None else (layer, direction)
    shape = (None,) * len(lead) + array.shape[len(lead) :]
    return pl.BlockSpec(shape, lambda i: lead + (0, 0))


def call(kernel, arrays, weights, outs, scratch):
    return pl.pallas_call(
        kernel,
        grid=(1,),
        in_specs=[whole(array.shape) for array in arrays] + [part_of(*entry) for entry in weights],
        out_specs=[whole(shape) for shape in outs],
        out_shape=[jax.ShapeDtypeStruct(shape, jnp.bfloat16) for shape in outs],
        scratch_shapes=scratch,
    )(*arrays, *[entry[0] for entry in weights])


def local_gathered(pair, w_query, w_key, w_value, w_gate, w_out, w_in, w_back):
    row_count = lax.axis_size("row")
    col_count = lax.axis_size("col")
    blocks, unused, span, width, channels = pair.shape
    inner = w_query.shape[3]
    pairs = row_count // 2
    length = blocks * width
    half = length // 2
    positions = half * length
    dims = (blocks, pairs, span, width)
    tile = pair.reshape(blocks, span, width, channels)
    w_value_gate = jnp.swapaxes(jnp.concatenate([w_value, w_gate], axis=3), 2, 3)

    def moved(array, dx, dc):
        if dx == 0:
            return lax.ppermute(array, "col", [(c, c ^ dc) for c in range(col_count)])
        if dc == 0:
            return lax.ppermute(array, "row", [(r, r ^ (2 * dx)) for r in range(row_count)])
        routes = []
        for r in range(row_count):
            for c in range(col_count):
                routes.append((r * col_count + c, (r ^ (2 * dx)) * col_count + (c ^ dc)))
        return lax.ppermute(array, ("row", "col"), routes)

    def to_partner(array):
        return lax.ppermute(array, "row", [(r, r ^ 1) for r in range(row_count)])

    near = jnp.stack([tile] + [moved(tile, 0, 2 * k) for k in range(1, blocks // 2)])
    parts = []
    for dx in range(pairs):
        for dy in range(2):
            parts.append(near if dx == dy == 0 else moved(near, dx, dy))

    f32, bf16 = jnp.float32, jnp.bfloat16
    grid = pltpu.VMEM((positions, channels), f32)
    stores = [
        pltpu.VMEM((positions, inner), bf16),
        pltpu.VMEM((positions, inner), bf16),
        pltpu.VMEM((inner, positions), bf16),
        pltpu.VMEM((inner, positions), f32),
    ]

    def attention(layer, direction):
        return [
            (w_query, layer, direction),
            (w_key, layer, direction),
            (w_value_gate, layer, direction),
            (w_out, layer, direction),
        ]

    quadrant = (half, half, channels)
    keep, send = call(
        functools.partial(first_row_kernel, dims),
        parts,
        attention(0, 0),
        [quadrant, quadrant],
        [grid] + stores,
    )
    layers = w_in.shape[0]
    for layer in range(layers - 1):
        slab, own, send = call(
            col_kernel,
            [keep, to_partner(send)],
            attention(layer, 1),
            [(half, length, channels), quadrant, quadrant],
            [grid] + stores,
        )
        last = layer == layers - 2
        few = (width + blocks * span, half, channels)
        keep, send = call(
            functools.partial(mid_row_kernel, dims),
            [slab, own, to_partner(send)],
            [(w_in, layer), (w_back, layer)] + attention(layer + 1, 0),
            [few, few],
            [grid] + stores,
        )
    layer = layers - 1
    seqs = width + blocks * span
    (result,) = call(
        functools.partial(last_kernel, dims),
        [keep, to_partner(send)],
        [
            (w_query, layer, 1),
            (w_key, layer, 1),
            (w_value, layer, 1),
            (w_gate, layer, 1),
            (w_out, layer, 1),
            (w_in, layer),
            (w_back, layer),
        ],
        [pair.shape],
        [
            pltpu.VMEM((seqs * length, channels), f32),
            pltpu.VMEM((seqs * length, inner), bf16),
            pltpu.VMEM((seqs * length, inner), bf16),
            pltpu.VMEM((2 * width * blocks * span, channels), f32),
            pltpu.VMEM((2 * width * blocks * span, inner), f32),
        ],
    )
    return result


def fits_gathered(mesh, pair, w_query, w_in):
    row_count, col_count = mesh.shape["row"], mesh.shape["col"]
    blocks, groups, span, total, channels = pair.shape
    width = total // col_count
    length = blocks * groups * span
    inner = w_query.shape[3]
    sizes_ok = (
        groups == row_count == 4
        and blocks == col_count
        and col_count & (col_count - 1) == 0
        and width == 8
        and 2 * length == LANES
        and channels == LANES
        and inner == HEADS * HEAD_DIM
        and w_in.shape[0] == 2
    )
    half = length * length // 2
    return sizes_ok and half * (4 * channels + 10 * inner) < VMEM_BUDGET


def solution(mesh):
    def run(*arrays):
        pair, w_query, w_in = arrays[0], arrays[1], arrays[6]
        body = local_gathered if fits_gathered(mesh, pair, w_query, w_in) else local_slabs
        return jax.shard_map(
            body,
            mesh=mesh,
            in_specs=(P(None, "row", None, "col", None), P(), P(), P(), P(), P(), P(), P()),
            out_specs=P(None, "row", None, "col", None),
            check_vma=False,
        )(*arrays)

    return run
```

```python
import functools
import math

import jax
import jax.numpy as jnp
from jax import lax
from jax.experimental import pallas as pl
from jax.experimental.pallas import tpu as pltpu
from jax.sharding import PartitionSpec as P

HEADS = 8
HEAD_DIM = 32
LANES = 128
SUBLANES = 8
VMEM_BUDGET = 24 * 2**20


epsilon = 1e-05


def layer_norm(values):
    wide = values.astype(jnp.float32)
    center = wide - jnp.mean(wide, axis=-1, keepdims=True)
    spread = jnp.mean(center * center, axis=-1, keepdims=True)
    return (center * lax.rsqrt(spread + epsilon)).astype(jnp.bfloat16)


def split_heads(matrix):
    return matrix.reshape(matrix.shape[0], HEADS, matrix.shape[1] // HEADS)


def attend(normed, weights, direction, pattern):
    project = pattern + ",chd->ehqd"
    queries = jnp.einsum(
        project, normed, split_heads(weights[0][direction]), preferred_element_type=jnp.float32
    ).astype(jnp.bfloat16)
    key_rows = jnp.einsum(
        project, normed, split_heads(weights[1][direction]), preferred_element_type=jnp.float32
    ).astype(jnp.bfloat16)
    value_rows = jnp.einsum(
        project, normed, split_heads(weights[2][direction]), preferred_element_type=jnp.float32
    ).astype(jnp.bfloat16)
    gating = jax.nn.sigmoid(
        jnp.einsum(
            project, normed, split_heads(weights[3][direction]), preferred_element_type=jnp.float32
        )
    )
    scores = jnp.einsum(
        "ehqd,ehkd->ehqk", queries, key_rows, preferred_element_type=jnp.float32
    ) * HEAD_DIM ** (-0.5)
    maximum = jnp.max(scores, axis=-1, keepdims=True)
    exponent = jnp.exp(scores - maximum)
    denominator = jnp.sum(exponent, axis=-1, keepdims=True)
    blended = (
        jnp.einsum(
            "ehqk,ehkd->ehqd",
            exponent.astype(jnp.bfloat16),
            value_rows,
            preferred_element_type=jnp.float32,
        )
        / denominator
    )
    gated_out = (gating * blended).astype(jnp.bfloat16)
    out_matrix = weights[4][direction]
    out_heads = out_matrix.reshape(HEADS, out_matrix.shape[0] // HEADS, out_matrix.shape[1])
    return jnp.einsum(
        "ehqd,hdc->" + pattern, gated_out, out_heads, preferred_element_type=jnp.float32
    )


def local_slabs(pair, w_query, w_key, w_value, w_gate, w_out, w_in, w_back):
    row_count = lax.axis_size("row")
    col_count = lax.axis_size("col")
    span_rows = pair.shape[2]
    col_width = pair.shape[3]
    channels = pair.shape[4]
    length = col_count * col_width
    pair_tile = pair.reshape(col_count, span_rows, col_width, channels)

    def layer_step(pair_tile, layer_weights):
        attn_weights = layer_weights[:5]
        row_slab = lax.all_to_all(
            pair_tile, "col", split_axis=0, concat_axis=2, tiled=True
        ).reshape(span_rows, length, channels)
        row_update = attend(layer_norm(row_slab), attn_weights, 0, "eqc")
        row_slab = (row_slab.astype(jnp.float32) + row_update).astype(jnp.bfloat16)
        pair_tile = lax.all_to_all(
            row_slab.reshape(1, span_rows, length, channels),
            "col",
            split_axis=2,
            concat_axis=0,
            tiled=True,
        )
        pair_tile = pair_tile.reshape(col_count, span_rows, row_count, span_rows, channels)
        col_slab = lax.all_to_all(pair_tile, "row", split_axis=2, concat_axis=1, tiled=True)
        col_slab = col_slab.reshape(length, span_rows, channels)
        col_update = attend(layer_norm(col_slab), attn_weights, 1, "qec")
        col_slab = (col_slab.astype(jnp.float32) + col_update).astype(jnp.bfloat16)
        pair_tile = lax.all_to_all(
            col_slab.reshape(col_count, row_count * span_rows, 1, span_rows, channels),
            "row",
            split_axis=1,
            concat_axis=2,
            tiled=True,
        )
        pair_tile = pair_tile.reshape(col_count, span_rows, col_width, channels)
        mirrored = lax.all_to_all(
            col_slab.reshape(col_count, col_width, span_rows, channels),
            "col",
            split_axis=0,
            concat_axis=2,
            tiled=True,
        )
        mirrored = jnp.transpose(
            mirrored.reshape(col_width, col_count * span_rows, channels), (1, 0, 2)
        )
        mirrored = mirrored.reshape(col_count, span_rows, col_width, channels)
        symmetric = (0.5 * (pair_tile.astype(jnp.float32) + mirrored.astype(jnp.float32))).astype(
            jnp.bfloat16
        )
        normed = layer_norm(symmetric)
        hidden = jax.nn.relu(
            jnp.einsum(
                "aewc,cf->aewf", normed, layer_weights[5], preferred_element_type=jnp.float32
            )
        ).astype(jnp.bfloat16)
        ff_out = jnp.einsum(
            "aewf,fc->aewc", hidden, layer_weights[6], preferred_element_type=jnp.float32
        )
        pair_tile = (symmetric.astype(jnp.float32) + ff_out).astype(jnp.bfloat16)
        return (pair_tile, None)

    final_tile, unused = lax.scan(
        layer_step, pair_tile, (w_query, w_key, w_value, w_gate, w_out, w_in, w_back)
    )
    return final_tile.reshape(pair.shape)


def dot(left, right, contract=((1,), (0,))):
    return lax.dot_general(left, right, (contract, ((), ())), preferred_element_type=jnp.float32)


NT = ((1,), (1,))
TN = ((0,), (0,))


def project(normed, span, weights, stores):
    w_key, w_rest = weights
    queries, keys, values, gates = stores[:4]
    inner = w_key.shape[1]
    keys[span, :] = dot(normed, w_key[...]).astype(jnp.bfloat16)
    queries[:, span] = dot(w_rest[:inner, :], normed, NT).astype(jnp.bfloat16)
    values[:, span] = dot(w_rest[inner : 2 * inner, :], normed, NT).astype(jnp.bfloat16)
    gates[:, span] = 0.5 * jnp.tanh(0.5 * dot(w_rest[2 * inner :, :], normed, NT)) + 0.5


def lane_halves(length):
    lane = lax.broadcasted_iota(jnp.int32, (1, 2 * LANES), 1) % LANES
    low = (lane < length).astype(jnp.float32).astype(jnp.bfloat16)
    high = (lane >= length).astype(jnp.float32).astype(jnp.bfloat16)
    return low, high


def softmax_tile(tile, start, length, stores, probs, inverses):
    queries, keys = stores[:2]
    low, high = lane_halves(length)
    scale = HEAD_DIM ** (-0.5) * math.log2(math.e)
    per_group = LANES // HEAD_DIM
    both = pl.ds(start, 2 * length)
    first_rows = pl.ds(start, length)
    second_rows = pl.ds(start + length, length)
    group = 2 * tile // per_group
    channels = slice(group * LANES, (group + 1) * LANES)
    key = jnp.concatenate([keys[first_rows, channels], keys[second_rows, channels]], axis=1)
    blank = jnp.zeros((HEAD_DIM, LANES), jnp.bfloat16)
    columns = []
    for head in (2 * tile, 2 * tile + 1):
        query = queries[head * HEAD_DIM : (head + 1) * HEAD_DIM, both]
        column = [blank] * (2 * per_group)
        column[head % per_group] = query * low[:, :LANES]
        column[per_group + head % per_group] = query * high[:, :LANES]
        columns.append(jnp.concatenate(column, axis=0))
    scores = dot(key, jnp.concatenate(columns, axis=1))
    exponent = jnp.exp2((scores - jnp.max(scores, axis=0, keepdims=True)) * scale)
    inverses[tile] = 1.0 / jnp.sum(exponent, axis=0, keepdims=True)
    probs[tile] = exponent.astype(jnp.bfloat16)


def blend_tile(tile, start, length, stores, probs, inverses):
    values, gates, gated = stores[2:5]
    low, high = lane_halves(length)
    both = pl.ds(start, 2 * length)
    inner = slice(2 * tile * HEAD_DIM, 2 * (tile + 1) * HEAD_DIM)
    prob, inverse = probs[tile], inverses[tile]
    blended = dot(values[inner, both], jnp.concatenate([prob * low, prob * high], axis=0))
    blended = jnp.concatenate(
        [
            blended[:HEAD_DIM, :LANES] * inverse[:, :LANES],
            blended[HEAD_DIM:, LANES:] * inverse[:, LANES:],
        ],
        axis=0,
    )
    gated[inner, both] = (gates[inner, both] * blended).astype(jnp.bfloat16)


def rounded(values):
    return values.astype(jnp.bfloat16).astype(jnp.float32)


def attend_slab(length, weights, stores):
    w_key, w_rest, w_out = weights
    gated, grid, turned, probs, inverses = stores[4:]
    half = grid.shape[0] // length
    project(layer_norm(grid[...]), pl.ds(0, grid.shape[0]), (w_key, w_rest), stores)
    for phase in (softmax_tile, blend_tile):
        for pair in range(half // 2):
            for tile in range(HEADS // 2):
                phase(tile, pair * 2 * length, length, stores, probs.at[pair], inverses.at[pair])
    result = grid[...] + dot(gated[...], w_out[...], TN)
    for seq in range(half):
        for at in range(length // SUBLANES):
            start = (at * half + seq) * SUBLANES
            row = seq * length + at * SUBLANES
            turned[start : start + SUBLANES, :] = result[row : row + SUBLANES]


def position(turned, half, at):
    start = (at // SUBLANES) * (half * SUBLANES) + at % SUBLANES
    return turned[pl.ds(start, half, stride=SUBLANES), :].astype(jnp.bfloat16)


def transition(values, w_in, w_back):
    hidden = jnp.maximum(dot(layer_norm(values), w_in[...]), 0.0).astype(jnp.bfloat16)
    return rounded(values + dot(hidden, w_back[...]))


def first_row_kernel(dims, *refs):
    blocks, pairs, span, width = dims
    parts = refs[:4]
    w_key, w_rest, w_out, keep, send = refs[4:9]
    stores = refs[9:]
    grid, turned = stores[5:7]
    row, col = lax.axis_index("row"), lax.axis_index("col")
    x, core = row // 2, row % 2
    length = blocks * width
    half = blocks * pairs * span
    for number, part in enumerate(parts):
        dx, dy = number // 2, number % 2
        at_x = x ^ dx
        for other in range(blocks // 2):
            at_c = col ^ (2 * other + dy)
            for a in range(blocks):
                for e in range(span):
                    at = ((a * pairs + at_x) * span + e) * length + at_c * width
                    grid[pl.ds(pl.multiple_of(at, width), width), :] = part[other, a, e].astype(
                        jnp.float32
                    )
    attend_slab(length, (w_key, w_rest, w_out), stores)
    for target, parity in ((keep, core), (send, 1 - core)):
        for a in range(blocks):
            for other in range(pairs):
                for e in range(span):
                    at = a * width + other * 2 * span + parity * span + e
                    target[(a * pairs + other) * span + e] = position(turned, half, at)


def col_kernel(keep, recv, w_key, w_rest, w_out, slab, own, send, *stores):
    grid, turned = stores[5:7]
    half = keep.shape[1]
    length = 2 * half
    both = jnp.concatenate([keep[...], recv[...]], axis=1).astype(jnp.float32)
    grid[...] = both.reshape(grid.shape)
    attend_slab(length, (w_key, w_rest, w_out), stores)
    groups = length // SUBLANES
    for j in range(half):
        for at in range(0, groups, 2):
            rows = [(at + k) * half * SUBLANES + j * SUBLANES for k in range(2)]
            slab[j, at * SUBLANES : (at + 2) * SUBLANES] = jnp.concatenate(
                [turned[row : row + SUBLANES, :] for row in rows], axis=0
            ).astype(jnp.bfloat16)
    for i in range(half):
        own[i] = position(turned, half, i)
        send[i] = position(turned, half, half + i)


def mid_row_kernel(
    dims, slab, own, recv, w_in, w_back, w_key, w_rest, w_out, keep, send, *stores
):
    grid, turned = stores[5:7]
    blocks, pairs, span, width = dims
    half = own.shape[0]
    length = 2 * half
    row, col = lax.axis_index("row"), lax.axis_index("col")
    x, core = row // 2, row % 2
    direct = jnp.concatenate([own[...], recv[...]], axis=1).astype(jnp.float32)
    values = rounded(0.5 * (direct + slab[...].astype(jnp.float32)))
    grid[...] = transition(values.reshape(grid.shape), w_in, w_back)
    attend_slab(length, (w_key, w_rest, w_out), stores)
    for other in range(pairs):
        for k in range(2):
            for e in range(span):
                number = (other * 2 + k) * span + e
                column = position(turned, half, half * (k ^ core) + (col * pairs + other) * span + e)
                keep[number] = column
                send[number] = column
    for a in range(blocks):
        for e in range(span):
            inside = (a * pairs + x) * span + e
            number = width + a * span + e
            keep[number] = position(turned, half, inside)
            send[number] = position(turned, half, half + inside)


def few_queries(query, keys, values, head_masks, tile_masks):
    scale = HEAD_DIM ** (-0.5) * math.log2(math.e)
    count = query.shape[0]
    spread = jnp.concatenate([query * mask for mask in head_masks], axis=0)
    scores = dot(spread, keys, NT)
    exponent = jnp.exp2((scores - jnp.max(scores, axis=1, keepdims=True)) * scale)
    denominator = jnp.sum(exponent, axis=1, keepdims=True)
    blended = dot(exponent.astype(jnp.bfloat16), values) / denominator
    total = None
    for h in range(HEADS):
        term = blended[h * count : (h + 1) * count] * tile_masks[h]
        total = term if total is None else total + term
    return total


def last_kernel(
    dims, keep, recv, w_query, w_key, w_value, w_gate, w_out, w_in, w_back, out, grid, keys, values, picked, blended
):
    blocks, pairs, span, width = dims
    half = keep.shape[1]
    length = 2 * half
    seqs = keep.shape[0]
    row, col = lax.axis_index("row"), lax.axis_index("col")
    x, core = row // 2, row % 2
    tall = blocks * span
    tile = width * tall
    chunk = 8
    for index in range(seqs // chunk):
        part = slice(index * chunk, (index + 1) * chunk)
        wide = jnp.concatenate([keep[part], recv[part]], axis=1).astype(jnp.float32)
        wide = wide.reshape(chunk * length, wide.shape[2])
        here = slice(index * chunk * length, (index + 1) * chunk * length)
        grid[here, :] = wide
        normed = layer_norm(wide)
        keys[here, :] = dot(normed, w_key[...]).astype(jnp.bfloat16)
        values[here, :] = dot(normed, w_value[...]).astype(jnp.bfloat16)
    for w in range(width):
        for e in range(span):
            at = w * length + x * span + e
            picked[pl.ds((w * span + e) * blocks, blocks), :] = grid[
                pl.ds(at, blocks, stride=pairs * span), :
            ]
    for a in range(blocks):
        for e in range(span):
            seq = width + a * span + e
            for other in range(pairs):
                for k in range(2):
                    for e2 in range(span):
                        w = (other * 2 + k) * span + e2
                        at = seq * length + half * (k ^ core) + (col * pairs + other) * span + e2
                        picked[pl.ds(tile + (e * blocks + a) * width + w, 1), :] = grid[
                            pl.ds(at, 1), :
                        ]
    here = picked[...]
    normed = layer_norm(here)
    queries = dot(normed, w_query[...]).astype(jnp.bfloat16)
    gating = jax.nn.sigmoid(dot(normed, w_gate[...]))
    inner = queries.shape[1]
    lane = lax.broadcasted_iota(jnp.int32, (1, inner), 1)
    tile_masks = [(lane // HEAD_DIM == h).astype(jnp.float32) for h in range(HEADS)]
    head_masks = [mask.astype(jnp.bfloat16) for mask in tile_masks]
    for w in range(width):
        rows = slice(w * tall, (w + 1) * tall)
        at = slice(w * length, (w + 1) * length)
        blended[rows, :] = few_queries(queries[rows], keys[at, :], values[at, :], head_masks, tile_masks)
    for a in range(blocks):
        for e in range(span):
            start = tile + (e * blocks + a) * width
            seq = width + a * span + e
            rows = slice(start, start + width)
            at = slice(seq * length, (seq + 1) * length)
            blended[rows, :] = few_queries(
                queries[rows], keys[at, :], values[at, :], head_masks, tile_masks
            )
    gated = (gating * blended[...]).astype(jnp.bfloat16)
    picked[...] = rounded(here + dot(gated, w_out[...]))
    for e in range(span):
        for a in range(blocks):
            start = (e * blocks + a) * width
            direct = picked[pl.ds(e * blocks + a, width, stride=tall), :]
            mirrored = picked[tile + start : tile + start + width, :]
            grid[start : start + width, :] = rounded(0.5 * (direct + mirrored))
    result = transition(grid[:tile, :], w_in, w_back)
    for e in range(span):
        for a in range(blocks):
            start = (e * blocks + a) * width
            out[a, 0, e] = result[start : start + width].astype(jnp.bfloat16)


def whole(shape):
    return pl.BlockSpec(shape, lambda i: (0,) * len(shape))


def part_of(array, layer, direction=None):
    lead = (layer,) if direction is None else (layer, direction)
    shape = (None,) * len(lead) + array.shape[len(lead) :]
    return pl.BlockSpec(shape, lambda i: lead + (0, 0))


def call(kernel, arrays, weights, outs, scratch):
    return pl.pallas_call(
        kernel,
        grid=(1,),
        in_specs=[whole(array.shape) for array in arrays] + [part_of(*entry) for entry in weights],
        out_specs=[whole(shape) for shape in outs],
        out_shape=[jax.ShapeDtypeStruct(shape, jnp.bfloat16) for shape in outs],
        scratch_shapes=scratch,
    )(*arrays, *[entry[0] for entry in weights])


def local_gathered(pair, w_query, w_key, w_value, w_gate, w_out, w_in, w_back):
    row_count = lax.axis_size("row")
    col_count = lax.axis_size("col")
    blocks, unused, span, width, channels = pair.shape
    inner = w_query.shape[3]
    pairs = row_count // 2
    length = blocks * width
    half = length // 2
    positions = half * length
    dims = (blocks, pairs, span, width)
    tile = pair.reshape(blocks, span, width, channels)
    w_rest = jnp.swapaxes(jnp.concatenate([w_query, w_value, w_gate], axis=3), 2, 3)

    def moved(array, dx, dc):
        if dx == 0:
            return lax.ppermute(array, "col", [(c, c ^ dc) for c in range(col_count)])
        if dc == 0:
            return lax.ppermute(array, "row", [(r, r ^ (2 * dx)) for r in range(row_count)])
        routes = []
        for r in range(row_count):
            for c in range(col_count):
                routes.append((r * col_count + c, (r ^ (2 * dx)) * col_count + (c ^ dc)))
        return lax.ppermute(array, ("row", "col"), routes)

    def to_partner(array):
        return lax.ppermute(array, "row", [(r, r ^ 1) for r in range(row_count)])

    near = jnp.stack([tile] + [moved(tile, 0, 2 * k) for k in range(1, blocks // 2)])
    parts = []
    for dx in range(pairs):
        for dy in range(2):
            parts.append(near if dx == dy == 0 else moved(near, dx, dy))

    f32, bf16 = jnp.float32, jnp.bfloat16
    stores = [
        pltpu.VMEM((inner, positions), bf16),
        pltpu.VMEM((positions, inner), bf16),
        pltpu.VMEM((inner, positions), bf16),
        pltpu.VMEM((inner, positions), f32),
        pltpu.VMEM((inner, positions), bf16),
        pltpu.VMEM((positions, channels), f32),
        pltpu.VMEM((positions, channels), f32),
        pltpu.VMEM((half // 2, HEADS // 2, length, 2 * LANES), bf16),
        pltpu.VMEM((half // 2, HEADS // 2, 1, 2 * LANES), f32),
    ]

    def attention(layer, direction):
        return [
            (w_key, layer, direction),
            (w_rest, layer, direction),
            (w_out, layer, direction),
        ]

    quadrant = (half, half, channels)
    keep, send = call(
        functools.partial(first_row_kernel, dims),
        parts,
        attention(0, 0),
        [quadrant, quadrant],
        stores,
    )
    layers = w_in.shape[0]
    for layer in range(layers - 1):
        slab, own, send = call(
            col_kernel,
            [keep, to_partner(send)],
            attention(layer, 1),
            [(half, length, channels), quadrant, quadrant],
            stores,
        )
        last = layer == layers - 2
        few = (width + blocks * span, half, channels)
        keep, send = call(
            functools.partial(mid_row_kernel, dims),
            [slab, own, to_partner(send)],
            [(w_in, layer), (w_back, layer)] + attention(layer + 1, 0),
            [few, few],
            stores,
        )
    layer = layers - 1
    seqs = width + blocks * span
    (result,) = call(
        functools.partial(last_kernel, dims),
        [keep, to_partner(send)],
        [
            (w_query, layer, 1),
            (w_key, layer, 1),
            (w_value, layer, 1),
            (w_gate, layer, 1),
            (w_out, layer, 1),
            (w_in, layer),
            (w_back, layer),
        ],
        [pair.shape],
        [
            pltpu.VMEM((seqs * length, channels), f32),
            pltpu.VMEM((seqs * length, inner), bf16),
            pltpu.VMEM((seqs * length, inner), bf16),
            pltpu.VMEM((2 * width * blocks * span, channels), f32),
            pltpu.VMEM((2 * width * blocks * span, inner), f32),
        ],
    )
    return result


def fits_gathered(mesh, pair, w_query, w_in):
    row_count, col_count = mesh.shape["row"], mesh.shape["col"]
    blocks, groups, span, total, channels = pair.shape
    width = total // col_count
    length = blocks * groups * span
    inner = w_query.shape[3]
    sizes_ok = (
        groups == row_count == 4
        and blocks == col_count
        and col_count & (col_count - 1) == 0
        and width == 8
        and 2 * length == LANES
        and channels == LANES
        and inner == HEADS * HEAD_DIM
        and w_in.shape[0] == 2
    )
    half = length * length // 2
    return sizes_ok and half * (4 * channels + 10 * inner) < VMEM_BUDGET


def solution(mesh):
    def run(*arrays):
        pair, w_query, w_in = arrays[0], arrays[1], arrays[6]
        body = local_gathered if fits_gathered(mesh, pair, w_query, w_in) else local_slabs
        return jax.shard_map(
            body,
            mesh=mesh,
            in_specs=(P(None, "row", None, "col", None), P(), P(), P(), P(), P(), P(), P()),
            out_specs=P(None, "row", None, "col", None),
            check_vma=False,
        )(*arrays)

    return run
```

```python
import functools
import math

import jax
import jax.numpy as jnp
from jax import lax
from jax.experimental import pallas as pl
from jax.experimental.pallas import tpu as pltpu
from jax.sharding import PartitionSpec as P

HEADS = 8
HEAD_DIM = 32
LANES = 128
SUBLANES = 8
VMEM_BUDGET = 24 * 2**20
VMEM_GRANT = 36 * 2**20


epsilon = 1e-05


def layer_norm(values):
    wide = values.astype(jnp.float32)
    center = wide - jnp.mean(wide, axis=-1, keepdims=True)
    spread = jnp.mean(center * center, axis=-1, keepdims=True)
    return (center * lax.rsqrt(spread + epsilon)).astype(jnp.bfloat16)


def split_heads(matrix):
    return matrix.reshape(matrix.shape[0], HEADS, matrix.shape[1] // HEADS)


def attend(normed, weights, direction, pattern):
    project = pattern + ",chd->ehqd"
    queries = jnp.einsum(
        project, normed, split_heads(weights[0][direction]), preferred_element_type=jnp.float32
    ).astype(jnp.bfloat16)
    key_rows = jnp.einsum(
        project, normed, split_heads(weights[1][direction]), preferred_element_type=jnp.float32
    ).astype(jnp.bfloat16)
    value_rows = jnp.einsum(
        project, normed, split_heads(weights[2][direction]), preferred_element_type=jnp.float32
    ).astype(jnp.bfloat16)
    gating = jax.nn.sigmoid(
        jnp.einsum(
            project, normed, split_heads(weights[3][direction]), preferred_element_type=jnp.float32
        )
    )
    scores = jnp.einsum(
        "ehqd,ehkd->ehqk", queries, key_rows, preferred_element_type=jnp.float32
    ) * HEAD_DIM ** (-0.5)
    maximum = jnp.max(scores, axis=-1, keepdims=True)
    exponent = jnp.exp(scores - maximum)
    denominator = jnp.sum(exponent, axis=-1, keepdims=True)
    blended = (
        jnp.einsum(
            "ehqk,ehkd->ehqd",
            exponent.astype(jnp.bfloat16),
            value_rows,
            preferred_element_type=jnp.float32,
        )
        / denominator
    )
    gated_out = (gating * blended).astype(jnp.bfloat16)
    out_matrix = weights[4][direction]
    out_heads = out_matrix.reshape(HEADS, out_matrix.shape[0] // HEADS, out_matrix.shape[1])
    return jnp.einsum(
        "ehqd,hdc->" + pattern, gated_out, out_heads, preferred_element_type=jnp.float32
    )


def local_slabs(pair, w_query, w_key, w_value, w_gate, w_out, w_in, w_back):
    row_count = lax.axis_size("row")
    col_count = lax.axis_size("col")
    span_rows = pair.shape[2]
    col_width = pair.shape[3]
    channels = pair.shape[4]
    length = col_count * col_width
    pair_tile = pair.reshape(col_count, span_rows, col_width, channels)

    def layer_step(pair_tile, layer_weights):
        attn_weights = layer_weights[:5]
        row_slab = lax.all_to_all(
            pair_tile, "col", split_axis=0, concat_axis=2, tiled=True
        ).reshape(span_rows, length, channels)
        row_update = attend(layer_norm(row_slab), attn_weights, 0, "eqc")
        row_slab = (row_slab.astype(jnp.float32) + row_update).astype(jnp.bfloat16)
        pair_tile = lax.all_to_all(
            row_slab.reshape(1, span_rows, length, channels),
            "col",
            split_axis=2,
            concat_axis=0,
            tiled=True,
        )
        pair_tile = pair_tile.reshape(col_count, span_rows, row_count, span_rows, channels)
        col_slab = lax.all_to_all(pair_tile, "row", split_axis=2, concat_axis=1, tiled=True)
        col_slab = col_slab.reshape(length, span_rows, channels)
        col_update = attend(layer_norm(col_slab), attn_weights, 1, "qec")
        col_slab = (col_slab.astype(jnp.float32) + col_update).astype(jnp.bfloat16)
        pair_tile = lax.all_to_all(
            col_slab.reshape(col_count, row_count * span_rows, 1, span_rows, channels),
            "row",
            split_axis=1,
            concat_axis=2,
            tiled=True,
        )
        pair_tile = pair_tile.reshape(col_count, span_rows, col_width, channels)
        mirrored = lax.all_to_all(
            col_slab.reshape(col_count, col_width, span_rows, channels),
            "col",
            split_axis=0,
            concat_axis=2,
            tiled=True,
        )
        mirrored = jnp.transpose(
            mirrored.reshape(col_width, col_count * span_rows, channels), (1, 0, 2)
        )
        mirrored = mirrored.reshape(col_count, span_rows, col_width, channels)
        symmetric = (0.5 * (pair_tile.astype(jnp.float32) + mirrored.astype(jnp.float32))).astype(
            jnp.bfloat16
        )
        normed = layer_norm(symmetric)
        hidden = jax.nn.relu(
            jnp.einsum(
                "aewc,cf->aewf", normed, layer_weights[5], preferred_element_type=jnp.float32
            )
        ).astype(jnp.bfloat16)
        ff_out = jnp.einsum(
            "aewf,fc->aewc", hidden, layer_weights[6], preferred_element_type=jnp.float32
        )
        pair_tile = (symmetric.astype(jnp.float32) + ff_out).astype(jnp.bfloat16)
        return (pair_tile, None)

    final_tile, unused = lax.scan(
        layer_step, pair_tile, (w_query, w_key, w_value, w_gate, w_out, w_in, w_back)
    )
    return final_tile.reshape(pair.shape)


def dot(left, right, contract=((1,), (0,))):
    return lax.dot_general(left, right, (contract, ((), ())), preferred_element_type=jnp.float32)


NT = ((1,), (1,))
TN = ((0,), (0,))


def project(normed, span, weights, stores):
    w_key, w_rest = weights
    queries, keys, values, gates = stores[:4]
    inner = w_key.shape[1]
    keys[span, :] = dot(normed, w_key[...]).astype(jnp.bfloat16)
    queries[:, span] = dot(w_rest[:inner, :], normed, NT).astype(jnp.bfloat16)
    values[:, span] = dot(w_rest[inner : 2 * inner, :], normed, NT).astype(jnp.bfloat16)
    gates[:, span] = 0.5 * jnp.tanh(0.5 * dot(w_rest[2 * inner :, :], normed, NT)) + 0.5


def lane_halves(length):
    lane = lax.broadcasted_iota(jnp.int32, (1, 2 * LANES), 1) % LANES
    low = (lane < length).astype(jnp.float32).astype(jnp.bfloat16)
    high = (lane >= length).astype(jnp.float32).astype(jnp.bfloat16)
    return low, high


def softmax_tile(tile, start, length, stores, probs, inverses):
    queries, keys = stores[:2]
    low, high = lane_halves(length)
    scale = HEAD_DIM ** (-0.5) * math.log2(math.e)
    per_group = LANES // HEAD_DIM
    both = pl.ds(start, 2 * length)
    first_rows = pl.ds(start, length)
    second_rows = pl.ds(start + length, length)
    group = 2 * tile // per_group
    channels = slice(group * LANES, (group + 1) * LANES)
    key = jnp.concatenate([keys[first_rows, channels], keys[second_rows, channels]], axis=1)
    blank = jnp.zeros((HEAD_DIM, LANES), jnp.bfloat16)
    columns = []
    for head in (2 * tile, 2 * tile + 1):
        query = queries[head * HEAD_DIM : (head + 1) * HEAD_DIM, both]
        column = [blank] * (2 * per_group)
        column[head % per_group] = query * low[:, :LANES]
        column[per_group + head % per_group] = query * high[:, :LANES]
        columns.append(jnp.concatenate(column, axis=0))
    scores = dot(key, jnp.concatenate(columns, axis=1))
    exponent = jnp.exp2((scores - jnp.max(scores, axis=0, keepdims=True)) * scale)
    inverses[tile] = 1.0 / jnp.sum(exponent, axis=0, keepdims=True)
    probs[tile] = exponent.astype(jnp.bfloat16)


def blend_tile(tile, start, length, stores, probs, inverses):
    values, gates, gated = stores[2:5]
    low, high = lane_halves(length)
    both = pl.ds(start, 2 * length)
    inner = slice(2 * tile * HEAD_DIM, 2 * (tile + 1) * HEAD_DIM)
    prob, inverse = probs[tile], inverses[tile]
    blended = dot(values[inner, both], jnp.concatenate([prob * low, prob * high], axis=0))
    blended = jnp.concatenate(
        [
            blended[:HEAD_DIM, :LANES] * inverse[:, :LANES],
            blended[HEAD_DIM:, LANES:] * inverse[:, LANES:],
        ],
        axis=0,
    )
    gated[inner, both] = (gates[inner, both] * blended).astype(jnp.bfloat16)


def rounded(values):
    return values.astype(jnp.bfloat16).astype(jnp.float32)


def attend_slab(length, weights, stores):
    w_key, w_rest, w_out = weights
    gated, grid, turned, probs, inverses = stores[4:]
    half = grid.shape[0] // length
    project(layer_norm(grid[...]), pl.ds(0, grid.shape[0]), (w_key, w_rest), stores)
    for phase in (softmax_tile, blend_tile):
        for pair in range(half // 2):
            for tile in range(HEADS // 2):
                phase(tile, pair * 2 * length, length, stores, probs.at[pair], inverses.at[pair])
    result = grid[...] + dot(gated[...], w_out[...], TN)
    for seq in range(half):
        for at in range(length // SUBLANES):
            start = (at * half + seq) * SUBLANES
            row = seq * length + at * SUBLANES
            turned[start : start + SUBLANES, :] = result[row : row + SUBLANES]


def position(turned, half, at):
    start = (at // SUBLANES) * (half * SUBLANES) + at % SUBLANES
    return turned[pl.ds(start, half, stride=SUBLANES), :].astype(jnp.bfloat16)


def transition(values, w_in, w_back):
    hidden = jnp.maximum(dot(layer_norm(values), w_in[...]), 0.0).astype(jnp.bfloat16)
    return rounded(values + dot(hidden, w_back[...]))


def first_row_kernel(dims, *refs):
    blocks, pairs, span, width = dims
    parts = refs[:4]
    w_key, w_rest, w_out, keep, send = refs[4:9]
    stores = refs[9:]
    grid, turned = stores[5:7]
    row, col = lax.axis_index("row"), lax.axis_index("col")
    x, core = row // 2, row % 2
    length = blocks * width
    half = blocks * pairs * span
    for number, part in enumerate(parts):
        dx, dy = number // 2, number % 2
        at_x = x ^ dx
        for other in range(blocks // 2):
            at_c = col ^ (2 * other + dy)
            for a in range(blocks):
                for e in range(span):
                    at = ((a * pairs + at_x) * span + e) * length + at_c * width
                    grid[pl.ds(pl.multiple_of(at, width), width), :] = part[other, a, e].astype(
                        jnp.float32
                    )
    attend_slab(length, (w_key, w_rest, w_out), stores)
    for target, parity in ((keep, core), (send, 1 - core)):
        for a in range(blocks):
            for other in range(pairs):
                for e in range(span):
                    at = a * width + other * 2 * span + parity * span + e
                    target[(a * pairs + other) * span + e] = position(turned, half, at)


def col_kernel(keep, recv, w_key, w_rest, w_out, slab, own, send, *stores):
    grid, turned = stores[5:7]
    half = keep.shape[1]
    length = 2 * half
    both = jnp.concatenate([keep[...], recv[...]], axis=1).astype(jnp.float32)
    grid[...] = both.reshape(grid.shape)
    attend_slab(length, (w_key, w_rest, w_out), stores)
    groups = length // SUBLANES
    for j in range(half):
        for at in range(0, groups, 2):
            rows = [(at + k) * half * SUBLANES + j * SUBLANES for k in range(2)]
            slab[j, at * SUBLANES : (at + 2) * SUBLANES] = jnp.concatenate(
                [turned[row : row + SUBLANES, :] for row in rows], axis=0
            ).astype(jnp.bfloat16)
    for i in range(half):
        own[i] = position(turned, half, i)
        send[i] = position(turned, half, half + i)


def mid_row_kernel(
    dims, slab, own, recv, w_in, w_back, w_key, w_rest, w_out, keep, send, *stores
):
    grid, turned = stores[5:7]
    blocks, pairs, span, width = dims
    half = own.shape[0]
    length = 2 * half
    row, col = lax.axis_index("row"), lax.axis_index("col")
    x, core = row // 2, row % 2
    direct = jnp.concatenate([own[...], recv[...]], axis=1).astype(jnp.float32)
    values = rounded(0.5 * (direct + slab[...].astype(jnp.float32)))
    grid[...] = transition(values.reshape(grid.shape), w_in, w_back)
    attend_slab(length, (w_key, w_rest, w_out), stores)
    for other in range(pairs):
        for k in range(2):
            for e in range(span):
                number = (other * 2 + k) * span + e
                column = position(turned, half, half * (k ^ core) + (col * pairs + other) * span + e)
                keep[number] = column
                send[number] = column
    for a in range(blocks):
        for e in range(span):
            inside = (a * pairs + x) * span + e
            number = width + a * span + e
            keep[number] = position(turned, half, inside)
            send[number] = position(turned, half, half + inside)


def few_queries(query, keys, values, head_masks, tile_masks):
    scale = HEAD_DIM ** (-0.5) * math.log2(math.e)
    count = query.shape[0]
    spread = jnp.concatenate([query * mask for mask in head_masks], axis=0)
    scores = dot(spread, keys, NT)
    exponent = jnp.exp2((scores - jnp.max(scores, axis=1, keepdims=True)) * scale)
    denominator = jnp.sum(exponent, axis=1, keepdims=True)
    blended = dot(exponent.astype(jnp.bfloat16), values) / denominator
    total = None
    for h in range(HEADS):
        term = blended[h * count : (h + 1) * count] * tile_masks[h]
        total = term if total is None else total + term
    return total


def last_kernel(
    dims, keep, recv, w_query, w_key, w_value, w_gate, w_out, w_in, w_back, out, grid, keys, values, picked, blended
):
    blocks, pairs, span, width = dims
    half = keep.shape[1]
    length = 2 * half
    seqs = keep.shape[0]
    row, col = lax.axis_index("row"), lax.axis_index("col")
    x, core = row // 2, row % 2
    tall = blocks * span
    tile = width * tall
    chunk = 8
    for index in range(seqs // chunk):
        part = slice(index * chunk, (index + 1) * chunk)
        wide = jnp.concatenate([keep[part], recv[part]], axis=1).astype(jnp.float32)
        wide = wide.reshape(chunk * length, wide.shape[2])
        here = slice(index * chunk * length, (index + 1) * chunk * length)
        grid[here, :] = wide
        normed = layer_norm(wide)
        keys[here, :] = dot(normed, w_key[...]).astype(jnp.bfloat16)
        values[here, :] = dot(normed, w_value[...]).astype(jnp.bfloat16)
    for w in range(width):
        for e in range(span):
            at = w * length + x * span + e
            picked[pl.ds((w * span + e) * blocks, blocks), :] = grid[
                pl.ds(at, blocks, stride=pairs * span), :
            ]
    for a in range(blocks):
        for e in range(span):
            seq = width + a * span + e
            for other in range(pairs):
                for k in range(2):
                    for e2 in range(span):
                        w = (other * 2 + k) * span + e2
                        at = seq * length + half * (k ^ core) + (col * pairs + other) * span + e2
                        picked[pl.ds(tile + (e * blocks + a) * width + w, 1), :] = grid[
                            pl.ds(at, 1), :
                        ]
    here = picked[...]
    normed = layer_norm(here)
    queries = dot(normed, w_query[...]).astype(jnp.bfloat16)
    gating = jax.nn.sigmoid(dot(normed, w_gate[...]))
    inner = queries.shape[1]
    lane = lax.broadcasted_iota(jnp.int32, (1, inner), 1)
    tile_masks = [(lane // HEAD_DIM == h).astype(jnp.float32) for h in range(HEADS)]
    head_masks = [mask.astype(jnp.bfloat16) for mask in tile_masks]
    for w in range(width):
        rows = slice(w * tall, (w + 1) * tall)
        at = slice(w * length, (w + 1) * length)
        blended[rows, :] = few_queries(queries[rows], keys[at, :], values[at, :], head_masks, tile_masks)
    for a in range(blocks):
        for e in range(span):
            start = tile + (e * blocks + a) * width
            seq = width + a * span + e
            rows = slice(start, start + width)
            at = slice(seq * length, (seq + 1) * length)
            blended[rows, :] = few_queries(
                queries[rows], keys[at, :], values[at, :], head_masks, tile_masks
            )
    gated = (gating * blended[...]).astype(jnp.bfloat16)
    picked[...] = rounded(here + dot(gated, w_out[...]))
    for e in range(span):
        for a in range(blocks):
            start = (e * blocks + a) * width
            direct = picked[pl.ds(e * blocks + a, width, stride=tall), :]
            mirrored = picked[tile + start : tile + start + width, :]
            grid[start : start + width, :] = rounded(0.5 * (direct + mirrored))
    result = transition(grid[:tile, :], w_in, w_back)
    for e in range(span):
        for a in range(blocks):
            start = (e * blocks + a) * width
            out[a, 0, e] = result[start : start + width].astype(jnp.bfloat16)


def whole(shape):
    return pl.BlockSpec(shape, lambda i: (0,) * len(shape))


def part_of(array, layer, direction=None):
    lead = (layer,) if direction is None else (layer, direction)
    shape = (None,) * len(lead) + array.shape[len(lead) :]
    return pl.BlockSpec(shape, lambda i: lead + (0, 0))


def call(kernel, arrays, weights, outs, scratch):
    return pl.pallas_call(
        kernel,
        grid=(1,),
        in_specs=[whole(array.shape) for array in arrays] + [part_of(*entry) for entry in weights],
        out_specs=[whole(shape) for shape in outs],
        out_shape=[jax.ShapeDtypeStruct(shape, jnp.bfloat16) for shape in outs],
        scratch_shapes=scratch,
        compiler_params=pltpu.CompilerParams(vmem_limit_bytes=VMEM_GRANT),
    )(*arrays, *[entry[0] for entry in weights])


def local_gathered(pair, w_query, w_key, w_value, w_gate, w_out, w_in, w_back):
    row_count = lax.axis_size("row")
    col_count = lax.axis_size("col")
    blocks, unused, span, width, channels = pair.shape
    inner = w_query.shape[3]
    pairs = row_count // 2
    length = blocks * width
    half = length // 2
    positions = half * length
    dims = (blocks, pairs, span, width)
    tile = pair.reshape(blocks, span, width, channels)
    w_rest = jnp.swapaxes(jnp.concatenate([w_query, w_value, w_gate], axis=3), 2, 3)

    def moved(array, dx, dc):
        if dx == 0:
            return lax.ppermute(array, "col", [(c, c ^ dc) for c in range(col_count)])
        if dc == 0:
            return lax.ppermute(array, "row", [(r, r ^ (2 * dx)) for r in range(row_count)])
        routes = []
        for r in range(row_count):
            for c in range(col_count):
                routes.append((r * col_count + c, (r ^ (2 * dx)) * col_count + (c ^ dc)))
        return lax.ppermute(array, ("row", "col"), routes)

    def to_partner(array):
        return lax.ppermute(array, "row", [(r, r ^ 1) for r in range(row_count)])

    near = jnp.stack([tile] + [moved(tile, 0, 2 * k) for k in range(1, blocks // 2)])
    parts = []
    for dx in range(pairs):
        for dy in range(2):
            parts.append(near if dx == dy == 0 else moved(near, dx, dy))

    f32, bf16 = jnp.float32, jnp.bfloat16
    stores = [
        pltpu.VMEM((inner, positions), bf16),
        pltpu.VMEM((positions, inner), bf16),
        pltpu.VMEM((inner, positions), bf16),
        pltpu.VMEM((inner, positions), f32),
        pltpu.VMEM((inner, positions), bf16),
        pltpu.VMEM((positions, channels), f32),
        pltpu.VMEM((positions, channels), f32),
        pltpu.VMEM((half // 2, HEADS // 2, length, 2 * LANES), bf16),
        pltpu.VMEM((half // 2, HEADS // 2, 1, 2 * LANES), f32),
    ]

    def attention(layer, direction):
        return [
            (w_key, layer, direction),
            (w_rest, layer, direction),
            (w_out, layer, direction),
        ]

    quadrant = (half, half, channels)
    keep, send = call(
        functools.partial(first_row_kernel, dims),
        parts,
        attention(0, 0),
        [quadrant, quadrant],
        stores,
    )
    layers = w_in.shape[0]
    for layer in range(layers - 1):
        slab, own, send = call(
            col_kernel,
            [keep, to_partner(send)],
            attention(layer, 1),
            [(half, length, channels), quadrant, quadrant],
            stores,
        )
        last = layer == layers - 2
        few = (width + blocks * span, half, channels)
        keep, send = call(
            functools.partial(mid_row_kernel, dims),
            [slab, own, to_partner(send)],
            [(w_in, layer), (w_back, layer)] + attention(layer + 1, 0),
            [few, few],
            stores,
        )
    layer = layers - 1
    seqs = width + blocks * span
    (result,) = call(
        functools.partial(last_kernel, dims),
        [keep, to_partner(send)],
        [
            (w_query, layer, 1),
            (w_key, layer, 1),
            (w_value, layer, 1),
            (w_gate, layer, 1),
            (w_out, layer, 1),
            (w_in, layer),
            (w_back, layer),
        ],
        [pair.shape],
        [
            pltpu.VMEM((seqs * length, channels), f32),
            pltpu.VMEM((seqs * length, inner), bf16),
            pltpu.VMEM((seqs * length, inner), bf16),
            pltpu.VMEM((2 * width * blocks * span, channels), f32),
            pltpu.VMEM((2 * width * blocks * span, inner), f32),
        ],
    )
    return result


def fits_gathered(mesh, pair, w_query, w_in):
    row_count, col_count = mesh.shape["row"], mesh.shape["col"]
    blocks, groups, span, total, channels = pair.shape
    width = total // col_count
    length = blocks * groups * span
    inner = w_query.shape[3]
    sizes_ok = (
        groups == row_count == 4
        and blocks == col_count
        and col_count & (col_count - 1) == 0
        and width == 8
        and 2 * length == LANES
        and channels == LANES
        and inner == HEADS * HEAD_DIM
        and w_in.shape[0] == 2
    )
    half = length * length // 2
    return sizes_ok and half * (4 * channels + 10 * inner) < VMEM_BUDGET


def solution(mesh):
    def run(*arrays):
        pair, w_query, w_in = arrays[0], arrays[1], arrays[6]
        body = local_gathered if fits_gathered(mesh, pair, w_query, w_in) else local_slabs
        return jax.shard_map(
            body,
            mesh=mesh,
            in_specs=(P(None, "row", None, "col", None), P(), P(), P(), P(), P(), P(), P()),
            out_specs=P(None, "row", None, "col", None),
            check_vma=False,
        )(*arrays)

    return run
```
